256 devices in a mesh: ket: 16 (over x, y_hi, core), bra: 16 (over z, y_lo).
Axes of the slice: x: 4, y: 4 (y_hi: 2, y_lo: 2; y = y_hi * 2 + y_lo), z: 8, core: 2. Of those that a mesh axis runs over, the one named last changes fastest.
Arguments:
- density: bfloat16 [2, 2, 12288, 12288], P(None, None, 'ket', 'bra'), may hold values from -6 to 6
- coupling: bfloat16 [48, 3, 256, 256], P('bra'), may hold values from -0.21875 to 0.21875
- block_cols: int32 [48, 3], replicated, may hold values from 0 to 47, as said below
- block_count: int32 [48], replicated, may hold values from 2 to 3, as said below
- energies: float32 [12288], replicated, may hold values from -0.5 to 97
Outputs:
- dissipated: bfloat16 [2, 2, 12288, 12288], P(None, None, 'ket', 'bra')
The draws below stay inside these ranges and needn't reach their ends.
Inputs may be any that keep to these rules, and one draw needn't show every extreme that they name: Row i of block_cols holds i - 1, i and i + 1 in some order; entries that would lie outside 0 to 47 stand last and are replaced by i. Slots k < block_count[i] name distinct blocks. block_count[i] is at most the number of block columns of i - 1, i, i + 1 inside the grid.
All inputs are finite; a program needn't handle non-finite values.
Results may differ from the reference program's by a relative error of at most 0.0054.
Values may be sent and summed in bfloat16 or wider, within the bound.
A program may use at most 320 MiB of HBM per device.

```python
import jax
import jax.numpy as jnp
from jax import lax

N = 12288
BS = 256
K = 3
R = 2
NB = 48


def block_pattern(key):
    block_total = N // BS
    positions = jnp.arange(block_total, dtype=jnp.int32)
    offsets = jnp.array([-1, 0, 1], dtype=jnp.int32)
    targets = positions[:, None] + offsets[None, :]
    usable = (targets >= 0) & (targets < block_total)
    scores = jax.random.randint(jax.random.fold_in(key, 29), (block_total, 3), 0, 1 << 20) * 4 + jnp.arange(3, dtype=jnp.int32)[None, :]
    scores = scores + (1 - usable.astype(jnp.int32)) * (1 << 24)
    ordering = jnp.argsort(scores, axis=1, stable=True)
    chosen = jnp.take_along_axis(targets, ordering, axis=1)
    chosen_usable = jnp.take_along_axis(usable, ordering, axis=1)
    columns = jnp.where(chosen_usable, chosen, positions[:, None])
    valid_level_count = jnp.sum(usable.astype(jnp.int32), axis=1)
    counts = jax.random.randint(jax.random.fold_in(key, 13), (block_total,), 2, 4)
    counts = counts.at[1].set(3)
    counts = jnp.minimum(counts, valid_level_count)
    return (columns.astype(jnp.int32), counts.astype(jnp.int32))


def draw_block_cols(key, part):
    return block_pattern(key)[0]


def draw_block_count(key, part):
    return block_pattern(key)[1]


def draw_energies(key, part):
    ramp = jnp.arange(N, dtype=jnp.float32) * (2.0 / BS)
    jitter = jax.random.uniform(jax.random.fold_in(key, 17), (N,), jnp.float32, -0.5, 0.5)
    return ramp + jitter


def steps_of(own_key, shape, cuts, least, high):
    factor_of, own = 1.0, jax.random.fold_in(own_key, 6)
    for dim, shards_of in cuts:
        heights = jnp.exp(jax.random.uniform(jax.random.fold_in(own, dim), (shards_of,), jnp.float32, least / len(cuts), high / len(cuts)))
        factor_of = factor_of * jnp.repeat(heights, shape[dim] // shards_of).reshape([-1 if axis == dim else 1 for axis in range(len(shape))])
    return factor_of


def scatter_about(stream_key, extent, scale, most, shards=(), held_as=jnp.bfloat16):
    drawn = jax.random.normal(stream_key, extent, jnp.float32) * scale
    if len(shards) > 0:
        drawn = steps_of(stream_key, extent, shards, -0.22, 0.18) * drawn
    return jnp.clip(drawn, min=-most, max=most).astype(held_as)


def setup_inputs(seed: int = 0) -> dict:
    key_list = jax.random.split(jax.random.key(seed), 6)
    return {
        "density": scatter_about(key_list[0], (R, 2, N, N), 1.0, 6.0, ((2, 16), (3, 16))),
        "coupling": scatter_about(key_list[1], (NB, K, BS, BS), (K * BS) ** -0.5, 0.21875, ((0, 16),)),
        "block_cols": draw_block_cols(jax.random.fold_in(key_list[5], 71), 0),
        "block_count": draw_block_count(jax.random.fold_in(key_list[5], 71), 0),
        "energies": draw_energies(jax.random.fold_in(key_list[5], 71), 0),
    }


thermal_beta_factor = 1.0
frequency_cutoff_scale = 4.0


def weigh(coupling, block_cols, block_count, energies):
    block_total = coupling.shape[0]
    slots = coupling.shape[1]
    block_size = coupling.shape[2]
    levels = energies.reshape(block_total, block_size)
    kept_levels = jnp.arange(slots, dtype=jnp.int32)[None, :] < block_count[:, None]
    col_levels = levels[block_cols]
    energy_detuning = levels[:, None, :, None] - col_levels[:, :, None, :]
    spectral_density = jax.nn.sigmoid(thermal_beta_factor * energy_detuning) * jnp.exp(-jnp.abs(energy_detuning) / frequency_cutoff_scale)
    held = kept_levels[:, :, None, None]
    operator = jnp.where(held, coupling, jnp.zeros_like(coupling))
    weighted = jnp.where(held, coupling.astype(jnp.float32) * spectral_density, jnp.float32(0.0)).astype(jnp.bfloat16)
    return operator, weighted


def reference(density, coupling, block_cols, block_count, energies):
    operator, weighted = weigh(coupling, block_cols, block_count, energies)
    copies, halves, states = density.shape[0], density.shape[1], density.shape[2]
    block_total = coupling.shape[0]
    block_size = coupling.shape[2]
    positions = jnp.arange(block_total, dtype=jnp.int32)

    def left_rows(matrix, source_blocks, block_row):
        picked = source_blocks[:, :, block_cols[block_row]]
        return jnp.einsum("kab,rpkbc->rpac", matrix[block_row].astype(jnp.float32), picked.astype(jnp.float32))

    def right_product_rows(matrix, source_operator, block_row):
        strip = lax.dynamic_slice_in_dim(source_operator, block_row * block_size, block_size, 2)
        pieces = strip.reshape(copies, halves, block_size, block_total, block_size)
        picked = pieces[:, :, :, block_cols]
        result = jnp.einsum("rpxjkb,jkab->rpxja", picked.astype(jnp.float32), matrix.astype(jnp.float32))
        return result.reshape(copies, halves, block_size, states)

    def assemble(blocks):
        return jnp.transpose(blocks, (1, 2, 0, 3, 4)).reshape(copies, halves, states, states)

    density_blocks = density.reshape(copies, halves, block_total, block_size, states)

    def commutand_row(block_row):
        return (left_rows(weighted, density_blocks, block_row) - right_product_rows(weighted, density, block_row)).astype(jnp.bfloat16)

    commutand = assemble(lax.map(commutand_row, positions))
    commutand_blocks = commutand.reshape(copies, halves, block_total, block_size, states)

    def dissipated_row(block_row):
        return (right_product_rows(operator, commutand, block_row) - left_rows(operator, commutand_blocks, block_row)).astype(jnp.bfloat16)

    return assemble(lax.map(dissipated_row, positions))
```

```python
import functools

import jax
import jax.numpy as jnp
from jax import lax
from jax.experimental import pallas as pl
from jax.experimental.pallas import tpu as pltpu
from jax.sharding import PartitionSpec as P

MESH = pl.DeviceIdType.MESH
BF = jnp.bfloat16
F32 = jnp.float32
CHAIN = 6
SWAP, CHAIN_R, CHAIN_L = 0, CHAIN, 2 * CHAIN
IN = CHAIN_L + CHAIN
DHALO = IN + 6
CHALO = DHALO + 12
OUT = CHALO + 8
COPIES = OUT + 6
ORDER = (0, 2, 1)


def kernel(nk, nb, density, panel, e_sub, e_lane, out, dext, cext, res, orow, ocol, wrow, wcol, ssem, rsem, lsem):
    bs = panel.shape[1]
    tile = density.shape[1]
    nr = tile // bs
    k, b = lax.axis_index("ket"), lax.axis_index("bra")
    core, hi, lo, z, nz = k % 2, (k // 2) % 2, b % 2, b // 2, nb // 2
    flip = b + 1 - 2 * lo
    colour = (hi + lo) % 2
    keep, give = 2 * colour, 2 - 2 * colour
    pair = (k, flip)
    swap = (k + 2 - 4 * hi, flip)
    up = ((k + nk - 1) % nk, core * b + (1 - core) * flip)
    down = ((k + 1) % nk, (1 - core) * b + core * flip)
    left, right = (k, (b + nb - 2) % nb), (k, (b + 2) % nb)
    dist = (z + nz - (k // 2) % nz) % nz

    def cols(half):
        return pl.ds(pl.multiple_of(bs + half * tile, bs), tile)

    mine, other = cols(lo), cols(1 - lo)
    first, last = pl.ds(bs, bs), pl.ds(nr * bs, bs)
    inner = pl.ds(bs, tile)
    above, below = pl.ds(0, bs), pl.ds((nr + 1) * bs, bs)
    lcol, rcol = pl.ds(bs, bs), pl.ds(2 * nr * bs, bs)
    lhalo, rhalo = pl.ds(0, bs), pl.ds((2 * nr + 1) * bs, bs)

    def remote(index, src, dst, device):
        return pltpu.make_async_remote_copy(
            src_ref=src, dst_ref=dst, send_sem=ssem.at[index], recv_sem=rsem.at[index],
            device_id=device, device_id_type=MESH,
        )

    own_tiles = [
        pltpu.make_async_copy(density.at[keep + m], dext.at[m, inner, mine], lsem.at[m]) for m in range(2)
    ]
    own_cols = pltpu.make_async_copy(panel, ocol.at[pl.ds(nr * lo, nr)], lsem.at[2])
    own_rows = pltpu.make_async_copy(ocol.at[pl.ds(nr * core, nr)], orow, lsem.at[3])
    for copy in own_tiles:
        copy.start()
    own_cols.start()

    barrier = pltpu.get_barrier_semaphore()
    for device in (pair, swap, up, down, left, right):
        pl.semaphore_signal(barrier, inc=1, device_id=device, device_id_type=MESH)
    pl.semaphore_wait(barrier, 6)

    part = nr * bs // CHAIN

    def piece(j):
        return j * part // bs, pl.ds(j * part % bs, part)

    swaps = []
    for j in range(CHAIN):
        row, where = piece(j)
        swaps.append(remote(SWAP + j, panel.at[row, where], ocol.at[nr * lo + row, where], swap))
        swaps[j].start()
    source = dist == 0
    swapped_source = source & (core != lo)

    def rows(r):
        return pl.ds(r * bs, bs)

    give_tiles = [
        [
            remote(IN + 3 * m + r, density.at[give + m, rows(r)], dext.at[m, rows(r + 1), mine], pair)
            for r in range(3)
        ]
        for m in range(2)
    ]

    halo = []
    for m in range(2):
        at = DHALO + 6 * m
        halo.append(
            [
                remote(at, density.at[keep + m, rows(0)], dext.at[m, below, mine], up),
                remote(at + 1, density.at[keep + m, rows(nr - 1)], dext.at[m, above, mine], down),
                remote(at + 2, dext.at[m, first, other], dext.at[m, below, other], up),
                remote(at + 3, dext.at[m, last, other], dext.at[m, above, other], down),
                remote(at + 4, dext.at[m, inner, lcol], dext.at[m, inner, rhalo], left),
                remote(at + 5, dext.at[m, inner, rcol], dext.at[m, inner, lhalo], right),
            ]
        )
    chalo = []
    for m in range(2):
        at = CHALO + 4 * m
        chalo.append(
            [
                remote(at, cext.at[m, first, pl.ds(bs, 2 * tile)], cext.at[m, below, pl.ds(bs, 2 * tile)], up),
                remote(at + 1, cext.at[m, last, pl.ds(bs, 2 * tile)], cext.at[m, above, pl.ds(bs, 2 * tile)], down),
                remote(at + 2, cext.at[m, inner, lcol], cext.at[m, inner, rhalo], left),
                remote(at + 3, cext.at[m, inner, rcol], cext.at[m, inner, lhalo], right),
            ]
        )

    def chain(j, act):
        row, where = piece(j)
        target = orow.at[row, where]

        def send(from_ref, index, device):
            return pltpu.make_async_remote_copy(
                src_ref=from_ref, dst_ref=target, send_sem=ssem.at[index + j], recv_sem=rsem.at[CHAIN_R + j],
                device_id=device, device_id_type=MESH,
            )

        on_right, on_left = send(target, CHAIN_R, right), send(target, CHAIN_L, left)
        held = ocol.at[nr * core + row, where]
        to_right = (dist != 0) & (dist < nz // 2)
        to_left = dist > nz // 2 + 1
        if act == "forward":

            @pl.when(swapped_source)
            def _():
                swaps[j].wait_recv()

            @pl.when(source)
            def _():
                send(held, CHAIN_R, right).start()
                send(held, CHAIN_L, left).start()

            @pl.when(dist != 0)
            def _():
                on_right.wait_recv()

            @pl.when(to_right)
            def _():
                on_right.start()

            @pl.when(to_left)
            def _():
                on_left.start()

        else:

            @pl.when(source | to_right)
            def _():
                on_right.wait_send()

            @pl.when(source | to_left)
            def _():
                on_left.wait_send()

    own_cols.wait()
    for r in ORDER:
        give_tiles[0][r].start()
    halo[0][0].start()
    halo[0][1].start()
    chain(0, "forward")
    chain(1, "forward")
    give_tiles[0][0].wait_recv()
    halo[0][2].start()
    chain(2, "forward")
    chain(3, "forward")
    give_tiles[0][2].wait_recv()
    halo[0][3].start()
    chain(4, "forward")
    chain(5, "forward")
    own_tiles[0].wait()
    give_tiles[0][1].wait_recv()
    halo[0][4].start()
    halo[0][5].start()
    for r in ORDER:
        give_tiles[0][r].wait_send()
    for r in ORDER:
        give_tiles[1][r].start()
    halo[1][0].start()
    halo[1][1].start()

    step = 32

    def weigh(source, target, index, at):
        def chunk(c, carry):
            where = pl.ds(pl.multiple_of(c * step, step), step)
            x = e_sub[at, where] - e_lane[at]
            u = jnp.exp(jnp.abs(x) * -0.25)
            q = u * u
            q = q * q
            spectral = jnp.where(x >= 0, 1.0, q) / (1.0 + q) * u
            target[index, where] = (source[index, where].astype(F32) * spectral).astype(BF)
            return carry

        lax.fori_loop(0, bs // step, chunk, 0)

    def weigh_all(source, target, count, offset):
        def one(p, carry):
            weigh(source, target, p, p + offset)
            return carry

        lax.fori_loop(0, count, one, 0)

    for j in range(CHAIN):

        @pl.when(jnp.logical_not(swapped_source))
        def _():
            swaps[j].wait_recv()

    @pl.when(source)
    def _():
        own_rows.start()
        own_rows.wait()

    weigh_all(orow, wrow, nr, 0)
    weigh_all(ocol, wcol, 2 * nr, nr)

    def block_row(m, i, source, row_op, col_op, sign, store):
        def half(h, carry):
            base = pl.multiple_of(h * tile, tile)
            through_rows = jnp.dot(
                row_op[i], source[m, pl.ds(i * bs, 3 * bs), pl.ds(pl.multiple_of(base + bs, bs), tile)],
                preferred_element_type=F32,
            )
            for j in range(nr):
                at = pl.multiple_of(base + j * bs, bs)
                through_cols = lax.dot_general(
                    source[m, rows(i + 1), pl.ds(at, 3 * bs)], col_op[h * nr + j],
                    (((1,), (1,)), ((), ())), preferred_element_type=F32,
                )
                store(m, i, at, (sign * (through_rows[:, j * bs : (j + 1) * bs] - through_cols)).astype(BF))
            return carry

        lax.fori_loop(0, 2, half, 0)

    def store_c(m, i, at, value):
        cext[m, rows(i + 1), pl.ds(pl.multiple_of(at + bs, bs), bs)] = value

    def store_out(m, i, at, value):
        res[m, rows(i), pl.ds(at, bs)] = value

    def commutand(m):
        for copy in halo[m]:
            copy.wait_recv()
        for i in ORDER:
            block_row(m, i, dext, wrow, wcol, 1.0, store_c)
            if i == 0:
                chalo[m][0].start()
            if i == nr - 1:
                chalo[m][1].start()
        chalo[m][2].start()
        chalo[m][3].start()

    def res_cols(half):
        return pl.ds(pl.multiple_of(half * tile, tile), tile)

    back = [
        [
            remote(OUT + 3 * m + i, res.at[m, rows(i), res_cols(1 - lo)], out.at[keep + m, rows(i)], pair)
            for i in range(3)
        ]
        for m in range(2)
    ]
    keep_out = [
        [
            pltpu.make_async_copy(res.at[m, rows(i), res_cols(lo)], out.at[keep + m, rows(i)], lsem.at[4 + 3 * m + i])
            for i in range(3)
        ]
        for m in range(2)
    ]

    def dissipated(m):
        for copy in chalo[m]:
            copy.wait_recv()
        for i in (1, 0, 2):
            block_row(m, i, cext, orow, ocol, -1.0, store_out)
            back[m][i].start()
            keep_out[m][i].start()

    commutand(0)
    own_tiles[1].wait()
    for r, at in ((0, (2,)), (2, (3,)), (1, (4, 5))):
        give_tiles[1][r].wait_recv()
        for a in at:
            halo[1][a].start()
    dissipated(0)
    commutand(1)
    dissipated(1)

    for j in range(CHAIN):
        swaps[j].wait_send()
        chain(j, "end")
    for r in range(3):
        give_tiles[1][r].wait_send()
    for m in range(2):
        for copy in halo[m] + chalo[m]:
            copy.wait_send()
        for i in range(3):
            keep_out[m][i].wait()
            back[m][i].wait_send()
            back[m][i].wait_recv()


def body(density, coupling, block_cols, block_count, energies):
    copies, halves, tile, _ = density.shape
    nr, slots, bs, _ = coupling.shape
    nk, nb = lax.axis_size("ket"), lax.axis_size("bra")
    k, b = lax.axis_index("ket"), lax.axis_index("bra")
    total = block_cols.shape[0]

    start = b * nr
    columns = lax.dynamic_slice_in_dim(block_cols, start, nr, 0)
    counts = lax.dynamic_slice_in_dim(block_count, start, nr, 0)
    used = jnp.arange(slots, dtype=jnp.int32)[None, :] < counts[:, None]
    place = columns - (start + jnp.arange(nr, dtype=jnp.int32))[:, None]
    zero = jnp.zeros((nr, bs, bs), coupling.dtype)
    blocks = []
    for offset in (-1, 0, 1):
        block = zero
        for s in range(slots):
            holds = (used[:, s] & (place[:, s] == offset))[:, None, None]
            block = jnp.where(holds, coupling[:, s], block)
        blocks.append(block)
    panel = jnp.concatenate(blocks, axis=2)

    levels = energies.reshape(total, bs)
    levels = jnp.concatenate([levels[:1], levels, levels[-1:]], axis=0)

    def level_sets(at, count):
        here = lax.dynamic_slice_in_dim(levels, at, count + 2, 0)
        return here[1 : count + 1], jnp.concatenate([here[:count], here[1 : count + 1], here[2:]], axis=1)

    row_sub, row_lane = level_sets(k * nr, nr)
    col_sub, col_lane = level_sets(b // 2 * 2 * nr, 2 * nr)
    e_sub = jnp.concatenate([row_sub, col_sub], axis=0)[:, :, None]
    e_lane = jnp.concatenate([row_lane, col_lane], axis=0)[:, None, :]

    any_space = pl.BlockSpec(memory_space=pl.ANY)
    vmem = pl.BlockSpec(memory_space=pltpu.VMEM)
    out = pl.pallas_call(
        functools.partial(kernel, nk, nb),
        out_shape=jax.ShapeDtypeStruct((copies * halves, tile, tile), density.dtype),
        in_specs=[any_space, any_space, vmem, vmem],
        out_specs=any_space,
        scratch_shapes=[
            pltpu.VMEM((2, tile + 2 * bs, 2 * tile + 2 * bs), BF),
            pltpu.VMEM((2, tile + 2 * bs, 2 * tile + 2 * bs), BF),
            pltpu.VMEM((2, tile, 2 * tile), BF),
            pltpu.VMEM((nr, bs, 3 * bs), BF),
            pltpu.VMEM((2 * nr, bs, 3 * bs), BF),
            pltpu.VMEM((nr, bs, 3 * bs), BF),
            pltpu.VMEM((2 * nr, bs, 3 * bs), BF),
            pltpu.SemaphoreType.DMA((COPIES,)),
            pltpu.SemaphoreType.DMA((COPIES,)),
            pltpu.SemaphoreType.DMA((10,)),
        ],
        compiler_params=pltpu.CompilerParams(
            collective_id=0, has_side_effects=True, vmem_limit_bytes=58 << 20
        ),
        name="dissipator",
    )(density.reshape(copies * halves, tile, tile), panel, e_sub, e_lane)
    return out.reshape(density.shape)


def solution(mesh):
    return jax.shard_map(
        body,
        mesh=mesh,
        in_specs=(P(None, None, "ket", "bra"), P("bra", None, None, None), P(), P(), P()),
        out_specs=P(None, None, "ket", "bra"),
        check_vma=False,
    )
```

```python
import functools

import jax
import jax.numpy as jnp
from jax import lax
from jax.experimental import pallas as pl
from jax.experimental.pallas import tpu as pltpu
from jax.sharding import PartitionSpec as P

MESH = pl.DeviceIdType.MESH
BF = jnp.bfloat16
F32 = jnp.float32
CHAIN = 6
SWAP = 0
RELAY = SWAP + CHAIN
RING = RELAY + CHAIN
IN = RING + CHAIN
DHALO = IN + 6
CHALO = DHALO + 12
OUT = CHALO + 8
COPIES = OUT + 6
ORDER = (0, 2, 1)
STEP = 32


def kernel(
    nk, nb, density, coupling, levels, block_cols, block_count, out,
    dext, cext, res, rraw, craw, orow, ocol, wrow, wcol, ssem, rsem, lsem,
):
    nr, slots, bs, _ = coupling.shape
    tile = nr * bs
    total = block_cols.shape[0]
    k, b = lax.axis_index("ket"), lax.axis_index("bra")
    core, hi, lo, z, nz = k % 2, (k // 2) % 2, b % 2, b // 2, nb // 2
    flip = b + 1 - 2 * lo
    colour = (hi + lo) % 2
    keep, give = 2 * colour, 2 - 2 * colour
    pair = (k, flip)
    swap = (k + 2 - 4 * hi, flip)
    sibling = (k + 1 - 2 * core, b)
    up = ((k + nk - 1) % nk, core * b + (1 - core) * flip)
    down = ((k + 1) % nk, (1 - core) * b + core * flip)
    left, right = (k, (b + nb - 2) % nb), (k, (b + 2) % nb)
    after = (k, (b + 2 + core * (nb - 4)) % nb)
    away = (z + nz - (k // 2) % nz) % nz
    dist = (away + core * (2 * nz - 2 * away)) % nz
    source = dist == 0
    swapped_source = source & (core != lo)

    def cols(half):
        return pl.ds(pl.multiple_of(bs + half * tile, bs), tile)

    def rows(r):
        return pl.ds(r * bs, bs)

    mine, other = cols(lo), cols(1 - lo)
    first, last = pl.ds(bs, bs), pl.ds(nr * bs, bs)
    inner, across = pl.ds(bs, tile), pl.ds(bs, 2 * tile)
    above, below = pl.ds(0, bs), pl.ds((nr + 1) * bs, bs)
    lcol, rcol = pl.ds(bs, bs), pl.ds(2 * nr * bs, bs)
    lhalo, rhalo = pl.ds(0, bs), pl.ds((2 * nr + 1) * bs, bs)

    def remote(sends, receives, src, dst, device):
        return pltpu.make_async_remote_copy(
            src_ref=src, dst_ref=dst, send_sem=ssem.at[sends], recv_sem=rsem.at[receives],
            device_id=device, device_id_type=MESH,
        )

    own_tiles = [
        pltpu.make_async_copy(density.at[keep + m], dext.at[m, inner, mine], lsem.at[m]) for m in range(2)
    ]
    own_cols = pltpu.make_async_copy(coupling, craw.at[pl.ds(nr * lo, nr)], lsem.at[2])
    own_rows = pltpu.make_async_copy(craw.at[pl.ds(nr * core, nr)], rraw, lsem.at[3])
    own_cols.start()
    for copy in own_tiles:
        copy.start()

    barrier = pltpu.get_barrier_semaphore()
    for device in (pair, swap, up, down, left, right):
        pl.semaphore_signal(barrier, inc=1, device_id=device, device_id_type=MESH)
    pl.semaphore_wait(barrier, 6)

    parts = CHAIN // nr
    part = bs // parts

    def piece(ref, base, j):
        return ref.at[base + j // parts, :, pl.ds(pl.multiple_of(j % parts * part, part), part)]

    def swap_copy(j):
        return remote(SWAP + j, SWAP + j, piece(coupling, 0, j), piece(craw, nr * lo, j), swap)

    def relay_copy(j):
        got = piece(craw, nr * (1 - lo), j)
        return remote(RELAY + j, SWAP + j, got, got, sibling)

    def ring_copy(j, start):
        target = piece(rraw, 0, j)
        return remote(RING + j, RING + j, piece(craw, nr * core, j) if start else target, target, after)

    give_tiles = [
        [
            remote(IN + 3 * m + r, IN + 3 * m + r, density.at[give + m, rows(r)], dext.at[m, rows(r + 1), mine], pair)
            for r in range(3)
        ]
        for m in range(2)
    ]

    halo, chalo = [], []
    for m in range(2):
        moves = (
            (density.at[keep + m, rows(0)], dext.at[m, below, mine], up),
            (density.at[keep + m, rows(nr - 1)], dext.at[m, above, mine], down),
            (dext.at[m, first, other], dext.at[m, below, other], up),
            (dext.at[m, last, other], dext.at[m, above, other], down),
            (dext.at[m, inner, lcol], dext.at[m, inner, rhalo], left),
            (dext.at[m, inner, rcol], dext.at[m, inner, lhalo], right),
        )
        halo.append([remote(DHALO + 6 * m + n, DHALO + 6 * m + n, *move) for n, move in enumerate(moves)])
        moves = (
            (cext.at[m, first, across], cext.at[m, below, across], up),
            (cext.at[m, last, across], cext.at[m, above, across], down),
            (cext.at[m, inner, lcol], cext.at[m, inner, rhalo], left),
            (cext.at[m, inner, rcol], cext.at[m, inner, lhalo], right),
        )
        chalo.append([remote(CHALO + 4 * m + n, CHALO + 4 * m + n, *move) for n, move in enumerate(moves)])

    def order_panel(raw, p, g, operator, weighted):
        coefs = [
            [
                ((block_cols[g, s] == g + o) & (s < block_count[g])).astype(jnp.int32).astype(F32)
                for s in range(slots)
            ]
            for o in (-1, 0, 1)
        ]
        here = jnp.transpose(jnp.broadcast_to(levels[pl.ds(g, 1), :], (128, bs)))
        for c in range(bs // STEP):
            at = pl.ds(c * STEP, STEP)
            held = [raw[p, s, at].astype(F32) for s in range(slots)]
            mine_levels = jnp.concatenate([here[c * STEP : (c + 1) * STEP]] * (bs // 128), axis=1)
            for n in range(3):
                there = levels[pl.ds((g + total + n - 1) % total, 1), :]
                x = mine_levels - there
                u = jnp.exp(jnp.abs(x) * -0.25)
                q = u * u
                q = q * q
                spectral = jnp.where(x >= 0, 1.0, q) / (1.0 + q) * u
                block = held[0] * coefs[n][0]
                for s in range(1, slots):
                    block = block + held[s] * coefs[n][s]
                operator[p, at, pl.ds(n * bs, bs)] = block.astype(BF)
                weighted[p, at, pl.ds(n * bs, bs)] = (block * spectral).astype(BF)

    col_start = b // 2 * 2 * nr

    def order_col(p):
        order_panel(craw, p, col_start + p, ocol, wcol)

    def service(s):
        j = s - dist
        active = (j >= 0) & (j < CHAIN)

        @pl.when((s < CHAIN) & (s % 2 == core))
        def _():
            swap_copy(s).wait_recv()
            relay_copy(s).start()

        @pl.when(swapped_source & (s < CHAIN) & (s % 2 != core))
        def _():
            swap_copy(s).wait_recv()

        @pl.when(active & source)
        def _():
            ring_copy(j, True).start()

        @pl.when(active & (dist != 0))
        def _():
            ring_copy(j, False).wait_recv()

        @pl.when(active & (dist != 0) & (dist < nz - 1))
        def _():
            ring_copy(j, False).start()

    def serve(begin, end, beside=None):
        def slot(s, carry):
            service(s)
            if beside is not None:
                beside(s - begin)
            return carry

        lax.fori_loop(begin, end, slot, 0)

    def taken(r, next_halo):
        give_tiles[0][r].wait_send()
        give_tiles[1][r].start()
        give_tiles[0][r].wait_recv()
        for n in next_halo:
            halo[0][n].start()

    for i in range(CHAIN // 2):
        swap_copy(2 * i + core).start()
    for r in ORDER:
        give_tiles[0][r].start()
    halo[0][0].start()
    halo[0][1].start()
    own_cols.wait()
    serve(0, 3)
    taken(0, (2,))
    serve(3, 6)
    taken(2, (3,))
    serve(6, 9, lambda p: order_col(nr * lo + p))
    own_tiles[0].wait()
    taken(1, (4, 5))
    halo[1][0].start()
    halo[1][1].start()
    for i in range(CHAIN // 2):

        @pl.when(jnp.logical_not(swapped_source))
        def _():
            swap_copy(2 * i + 1 - core).wait_recv()

    serve(9, 12, lambda p: order_col(nr * (1 - lo) + p))
    serve(12, max(13, CHAIN + nz - 1))

    @pl.when(source)
    def _():
        own_rows.start()
        own_rows.wait()

    def block_half(m, i, h, source_ref, row_op, col_op, store):
        base = pl.multiple_of(h * tile, tile)
        through_rows = jnp.dot(
            row_op[i], source_ref[m, pl.ds(i * bs, 3 * bs), pl.ds(pl.multiple_of(base + bs, bs), tile)],
            preferred_element_type=F32,
        )
        for j in range(nr):
            at = pl.multiple_of(base + j * bs, bs)
            through_cols = lax.dot_general(
                source_ref[m, rows(i + 1), pl.ds(at, 3 * bs)], col_op[h * nr + j],
                (((1,), (1,)), ((), ())), preferred_element_type=F32,
            )
            store(j, through_rows[:, j * bs : (j + 1) * bs], through_cols)

    def commutand_row(m, i):
        def half(h, carry):
            def store(j, through_rows, through_cols):
                at = pl.multiple_of(h * tile + (j + 1) * bs, bs)
                cext[m, rows(i + 1), pl.ds(at, bs)] = (through_rows - through_cols).astype(BF)

            block_half(m, i, h, dext, wrow, wcol, store)
            return carry

        lax.fori_loop(0, 2, half, 0)

    back = [
        [
            remote(OUT + 3 * m + i, OUT + 3 * m + i, res.at[m, rows(i)], out.at[keep + m, rows(i)], pair)
            for i in range(3)
        ]
        for m in range(2)
    ]

    def dissipated_row(m, i):
        def store_other(j, through_rows, through_cols):
            res[m, rows(i), rows(j)] = (through_cols - through_rows).astype(BF)

        def store_mine(j, through_rows, through_cols):
            out[keep + m, rows(i), rows(j)] = (through_cols - through_rows).astype(BF)

        block_half(m, i, 1 - lo, cext, orow, ocol, store_other)
        back[m][i].start()
        block_half(m, i, lo, cext, orow, ocol, store_mine)

    def commutand(m):
        for copy in halo[m]:
            copy.wait_recv()
        for n, i in enumerate(ORDER):
            if m == 0:
                order_panel(rraw, i, k * nr + i, orow, wrow)
            commutand_row(m, i)
            if n < 2:
                chalo[m][n].start()
        chalo[m][2].start()
        chalo[m][3].start()

    def dissipated(m):
        chalo[m][2].wait_recv()
        chalo[m][3].wait_recv()
        dissipated_row(m, 1)
        chalo[m][1].wait_recv()
        dissipated_row(m, 0)
        chalo[m][0].wait_recv()
        dissipated_row(m, 2)

    commutand(0)
    own_tiles[1].wait()
    for r, which in ((0, (2,)), (2, (3,)), (1, (4, 5))):
        give_tiles[1][r].wait_recv()
        for n in which:
            halo[1][n].start()
    dissipated(0)
    commutand(1)
    dissipated(1)

    for i in range(CHAIN // 2):
        swap_copy(2 * i + core).wait_send()
        relay_copy(2 * i + core).wait_send()
    for j in range(CHAIN):

        @pl.when(dist < nz - 1)
        def _():
            ring_copy(j, False).wait_send()

    for r in range(3):
        give_tiles[1][r].wait_send()
    for m in range(2):
        for copy in halo[m] + chalo[m]:
            copy.wait_send()
        for i in range(3):
            back[m][i].wait_send()
            back[m][i].wait_recv()


def body(density, coupling, block_cols, block_count, energies):
    copies, halves, tile, _ = density.shape
    nr, slots, bs, _ = coupling.shape
    nk, nb = lax.axis_size("ket"), lax.axis_size("bra")
    total = block_cols.shape[0]
    any_space = pl.BlockSpec(memory_space=pl.ANY)
    vmem = pl.BlockSpec(memory_space=pltpu.VMEM)
    smem = pl.BlockSpec(memory_space=pltpu.SMEM)
    out = pl.pallas_call(
        functools.partial(kernel, nk, nb),
        out_shape=pltpu.VMEM((copies * halves, tile, tile), density.dtype),
        in_specs=[any_space, any_space, vmem, smem, smem],
        out_specs=vmem,
        scratch_shapes=[
            pltpu.VMEM((2, tile + 2 * bs, 2 * tile + 2 * bs), BF),
            pltpu.VMEM((2, tile + 2 * bs, 2 * tile + 2 * bs), BF),
            pltpu.VMEM((2, tile, tile), BF),
            pltpu.VMEM((nr, slots, bs, bs), BF),
            pltpu.VMEM((2 * nr, slots, bs, bs), BF),
            pltpu.VMEM((nr, bs, 3 * bs), BF),
            pltpu.VMEM((2 * nr, bs, 3 * bs), BF),
            pltpu.VMEM((nr, bs, 3 * bs), BF),
            pltpu.VMEM((2 * nr, bs, 3 * bs), BF),
            pltpu.SemaphoreType.DMA((COPIES,)),
            pltpu.SemaphoreType.DMA((COPIES,)),
            pltpu.SemaphoreType.DMA((4,)),
        ],
        compiler_params=pltpu.CompilerParams(
            collective_id=0, has_side_effects=True, vmem_limit_bytes=52 << 20
        ),
        name="dissipator",
    )(density.reshape(copies * halves, tile, tile), coupling, energies.reshape(total, bs), block_cols, block_count)
    return out.reshape(density.shape)


def solution(mesh):
    return jax.shard_map(
        body,
        mesh=mesh,
        in_specs=(P(None, None, "ket", "bra"), P("bra", None, None, None), P(), P(), P()),
        out_specs=P(None, None, "ket", "bra"),
        check_vma=False,
    )
```

```python
import functools

import jax
import jax.numpy as jnp
from jax import lax
from jax.experimental import pallas as pl
from jax.experimental.pallas import tpu as pltpu
from jax.sharding import PartitionSpec as P

MESH = pl.DeviceIdType.MESH
BF = jnp.bfloat16
F32 = jnp.float32
CHAIN = 24
SWAP = 0
RELAY = SWAP + CHAIN
RING = RELAY + CHAIN
IN = RING + CHAIN
DHALO = IN + 6
CHALO = DHALO + 12
OUT = CHALO + 8
COPIES = OUT + 12
ORDER = (0, 2, 1)


def kernel(
    nk, nb, density, coupling, levels, block_cols, block_count, out,
    dext, cext, res, rraw, craw, orow, ocol, wrow, wcol, own_levels, ssem, rsem, lsem,
):
    nr, slots, bs, _ = coupling.shape
    tile = nr * bs
    total = block_cols.shape[0]
    k, b = lax.axis_index("ket"), lax.axis_index("bra")
    core, hi, lo, z, nz = k % 2, (k // 2) % 2, b % 2, b // 2, nb // 2
    flip = b + 1 - 2 * lo
    colour = (hi + lo) % 2
    keep, give = 2 * colour, 2 - 2 * colour
    pair = (k, flip)
    swap = (k + 2 - 4 * hi, flip)
    sibling = (k + 1 - 2 * core, b)
    up = ((k + nk - 1) % nk, core * b + (1 - core) * flip)
    down = ((k + 1) % nk, (1 - core) * b + core * flip)
    left, right = (k, (b + nb - 2) % nb), (k, (b + 2) % nb)
    after = (k, (b + 2 + core * (nb - 4)) % nb)
    away = (z + nz - (k // 2) % nz) % nz
    dist = (away + core * (2 * nz - 2 * away)) % nz
    source = dist == 0

    def cols(half):
        return pl.ds(pl.multiple_of(bs + half * tile, bs), tile)

    def rows(r):
        return pl.ds(r * bs, bs)

    mine, other = cols(lo), cols(1 - lo)
    first, last = pl.ds(bs, bs), pl.ds(nr * bs, bs)
    inner, across = pl.ds(bs, tile), pl.ds(bs, 2 * tile)
    above, below = pl.ds(0, bs), pl.ds((nr + 1) * bs, bs)
    lcol, rcol = pl.ds(bs, bs), pl.ds(2 * nr * bs, bs)
    lhalo, rhalo = pl.ds(0, bs), pl.ds((2 * nr + 1) * bs, bs)

    def remote(sends, receives, src, dst, device):
        return pltpu.make_async_remote_copy(
            src_ref=src, dst_ref=dst, send_sem=ssem.at[sends], recv_sem=rsem.at[receives],
            device_id=device, device_id_type=MESH,
        )

    own_tiles = [
        pltpu.make_async_copy(density.at[keep + m], dext.at[m, inner, mine], lsem.at[m]) for m in range(2)
    ]
    own_cols = pltpu.make_async_copy(coupling, craw.at[pl.ds(nr * lo, nr)], lsem.at[2])
    own_rows = pltpu.make_async_copy(craw.at[pl.ds(nr * core, nr)], rraw, lsem.at[3])
    own_cols.start()
    for copy in own_tiles:
        copy.start()

    barrier = pltpu.get_barrier_semaphore()
    for device in (pair, swap, up, down, left, right):
        pl.semaphore_signal(barrier, inc=1, device_id=device, device_id_type=MESH)

    col_start = b // 2 * 2 * nr
    for p in range(3 * nr):
        g = k * nr + p if p < nr else col_start + p - nr
        own_levels[p] = jnp.transpose(jnp.broadcast_to(levels[pl.ds(g, 1), :], (128, bs)))
    pl.semaphore_wait(barrier, 6)

    parts = CHAIN // nr
    part = bs // parts

    def block_row(j):
        return j // parts * 2 % 3

    def chunk_rows(j):
        return pl.ds(pl.multiple_of(j % parts * part, part), part)

    def piece(ref, base, j):
        return ref.at[base + block_row(j), :, chunk_rows(j)]

    def swap_copy(j):
        return remote(SWAP + j, SWAP + j, piece(coupling, 0, j), piece(craw, nr * lo, j), swap)

    def relay_copy(j):
        got = piece(craw, nr * (1 - lo), j)
        return remote(RELAY + j, SWAP + j, got, got, sibling)

    def ring_copy(j, start):
        target = piece(rraw, 0, j)
        return remote(RING + j, RING + j, piece(craw, nr * core, j) if start else target, target, after)

    give_tiles = [
        [
            remote(IN + 3 * m + r, IN + 3 * m + r, density.at[give + m, rows(r)], dext.at[m, rows(r + 1), mine], pair)
            for r in range(3)
        ]
        for m in range(2)
    ]

    halo, chalo = [], []
    for m in range(2):
        moves = (
            (density.at[keep + m, rows(0)], dext.at[m, below, mine], up),
            (density.at[keep + m, rows(nr - 1)], dext.at[m, above, mine], down),
            (dext.at[m, first, other], dext.at[m, below, other], up),
            (dext.at[m, last, other], dext.at[m, above, other], down),
            (dext.at[m, inner, lcol], dext.at[m, inner, rhalo], left),
            (dext.at[m, inner, rcol], dext.at[m, inner, lhalo], right),
        )
        halo.append([remote(DHALO + 6 * m + n, DHALO + 6 * m + n, *move) for n, move in enumerate(moves)])
        moves = (
            (cext.at[m, first, across], cext.at[m, below, across], up),
            (cext.at[m, last, across], cext.at[m, above, across], down),
            (cext.at[m, inner, lcol], cext.at[m, inner, rhalo], left),
            (cext.at[m, inner, rcol], cext.at[m, inner, lhalo], right),
        )
        chalo.append([remote(CHALO + 4 * m + n, CHALO + 4 * m + n, *move) for n, move in enumerate(moves)])

    def order_chunk(raw, p, g, q, operator, weighted, at):
        held = [raw[p, s, at].astype(F32) for s in range(slots)]
        mine_levels = jnp.concatenate([own_levels[q, at]] * (bs // 128), axis=1)
        for n in range(3):
            there = levels[pl.ds((g + total + n - 1) % total, 1), :]
            x = mine_levels - there
            u = jnp.exp(jnp.abs(x) * -0.25)
            v = u * u
            v = v * v
            spectral = jnp.where(x >= 0, 1.0, v) / (1.0 + v) * u
            block = None
            for s in range(slots):
                used = (block_cols[g, s] == g + n - 1) & (s < block_count[g])
                term = held[s] * used.astype(jnp.int32).astype(F32)
                block = term if block is None else block + term
            operator[p, at, pl.ds(n * bs, bs)] = block.astype(BF)
            weighted[p, at, pl.ds(n * bs, bs)] = (block * spectral).astype(BF)

    def order_col(half, j):
        p = half * nr + block_row(j)
        order_chunk(craw, p, col_start + p, nr + p, ocol, wcol, chunk_rows(j))

    def order_row(j):
        p = block_row(j)
        order_chunk(rraw, p, k * nr + p, p, orow, wrow, chunk_rows(j))

    def taken(r, next_halo):
        give_tiles[0][r].wait_recv()
        for n in next_halo:
            halo[0][n].start()

    def due(j, at):
        return (j == at) | ((j == 0) & (at < 0)) | ((j == CHAIN) & (at > CHAIN))

    near = dist < nz // 2
    ready_source = source & (core == lo)

    def first_taken():
        halo[0][0].start()
        halo[0][1].start()
        taken(0, (2,))

    def relay_step(i, carry):
        @pl.when(i == CHAIN // 4)
        def _():
            first_taken()

        swap_copy(2 * i + core).wait_recv()
        relay_copy(2 * i + core).start()
        order_col(lo, 2 * i)
        order_col(lo, 2 * i + 1)
        return carry

    def step(j, carry):
        @pl.when(near & due(j, 12 - 5 * dist))
        def _():
            first_taken()

        @pl.when(due(j, 28 - 5 * dist))
        def _():
            taken(2, (3,))

        @pl.when(due(j, 44 - 5 * dist))
        def _():
            own_tiles[0].wait()
            taken(1, (4, 5))
            halo[1][0].start()
            halo[1][1].start()

        @pl.when(j < CHAIN)
        def _():
            @pl.when(ready_source)
            def _():
                ring_copy(j, True).start()

            @pl.when((near & (j % 2 == core)) | (jnp.logical_not(ready_source) & (j % 2 != core)))
            def _():
                swap_copy(j).wait_recv()

            @pl.when(near & (j % 2 == core))
            def _():
                relay_copy(j).start()

            @pl.when(source & (core != lo))
            def _():
                ring_copy(j, True).start()

            @pl.when(jnp.logical_not(ready_source))
            def _():
                order_col(1 - lo, j)

            @pl.when(dist != 0)
            def _():
                ring_copy(j, False).wait_recv()

            @pl.when((dist != 0) & (dist < nz - 1))
            def _():
                ring_copy(j, False).start()

            @pl.when(dist != 0)
            def _():
                order_row(j)

        return carry

    for i in range(CHAIN // 2):
        swap_copy(2 * i + core).start()
    for m in range(2):
        for r in ORDER:
            give_tiles[m][r].start()
    own_cols.wait()

    @pl.when(jnp.logical_not(near))
    def _():
        lax.fori_loop(0, CHAIN // 2, relay_step, 0)

    lax.fori_loop(0, CHAIN + 1, step, 0)

    @pl.when(near)
    def _():
        def own_col_step(j, carry):
            order_col(lo, j)
            return carry

        lax.fori_loop(0, CHAIN, own_col_step, 0)

    @pl.when(ready_source)
    def _():
        def other_col_step(j, carry):
            @pl.when(j % 2 != core)
            def _():
                swap_copy(j).wait_recv()

            order_col(1 - lo, j)
            return carry

        lax.fori_loop(0, CHAIN, other_col_step, 0)

    @pl.when(source)
    def _():
        own_rows.start()
        own_rows.wait()

        def own_step(j, carry):
            order_row(j)
            return carry

        lax.fori_loop(0, CHAIN, own_step, 0)

    def blocks(m, i, h, c, count, source_ref, row_op, col_op, store):
        base = pl.multiple_of((h * nr + c) * bs, bs)
        through_rows = jnp.dot(
            row_op[i], source_ref[m, pl.ds(i * bs, 3 * bs), pl.ds(pl.multiple_of(base + bs, bs), count * bs)],
            preferred_element_type=F32,
        )
        for j in range(count):
            through_cols = lax.dot_general(
                source_ref[m, rows(i + 1), pl.ds(pl.multiple_of(base + j * bs, bs), 3 * bs)], col_op[h * nr + c + j],
                (((1,), (1,)), ((), ())), preferred_element_type=F32,
            )
            store(j, through_rows[:, j * bs : (j + 1) * bs], through_cols)

    def commutand_row(m, i):
        def half(h, carry):
            def store(j, through_rows, through_cols):
                at = pl.multiple_of(h * tile + (j + 1) * bs, bs)
                cext[m, rows(i + 1), pl.ds(at, bs)] = (through_rows - through_cols).astype(BF)

            blocks(m, i, h, 0, nr, dext, wrow, wcol, store)
            return carry

        lax.fori_loop(0, 2, half, 0)

    inside, edge = pl.ds(pl.multiple_of(lo * bs, bs), 2 * bs), pl.ds(pl.multiple_of(2 * (1 - lo) * bs, bs), bs)
    back = [
        [
            [
                remote(OUT + n, OUT + n, res.at[m, rows(i), where], out.at[keep + m, rows(i), where], pair)
                for n, where in ((6 * m + 2 * i, inside), (6 * m + 2 * i + 1, edge))
            ]
            for i in range(3)
        ]
        for m in range(2)
    ]

    def to_pair(m, i, at_edge):
        start = 2 * (1 - lo) if at_edge else lo

        def store(j, through_rows, through_cols):
            at = pl.multiple_of((start + j) * bs, bs)
            res[m, rows(i), pl.ds(at, bs)] = (through_cols - through_rows).astype(BF)

        blocks(m, i, 1 - lo, start, 1 if at_edge else 2, cext, orow, ocol, store)
        back[m][i][at_edge].start()

    def to_own(m, i):
        def store(j, through_rows, through_cols):
            out[keep + m, rows(i), rows(j)] = (through_cols - through_rows).astype(BF)

        blocks(m, i, lo, 0, nr, cext, orow, ocol, store)

    def row_to_pair(m, i):
        to_pair(m, i, 0)
        to_pair(m, i, 1)

    def give_on(r, which):
        give_tiles[1][r].wait_recv()
        for n in which:
            halo[1][n].start()

    for copy in halo[0]:
        copy.wait_recv()
    commutand_row(0, 0)
    chalo[0][0].start()
    commutand_row(0, 2)
    chalo[0][1].start()
    commutand_row(0, 1)
    chalo[0][2].start()
    chalo[0][3].start()
    give_on(0, (2,))
    give_on(2, (3,))
    to_pair(0, 1, 0)
    own_tiles[1].wait()
    give_on(1, (4, 5))
    chalo[0][2].wait_recv()
    chalo[0][3].wait_recv()
    to_pair(0, 1, 1)
    to_own(0, 1)
    chalo[0][1].wait_recv()
    row_to_pair(0, 0)
    for copy in halo[1]:
        copy.wait_recv()
    commutand_row(1, 0)
    chalo[1][0].start()
    chalo[0][0].wait_recv()
    row_to_pair(0, 2)
    commutand_row(1, 2)
    chalo[1][1].start()
    commutand_row(1, 1)
    chalo[1][2].start()
    chalo[1][3].start()
    to_pair(1, 1, 0)
    to_own(0, 0)
    to_own(0, 2)
    chalo[1][2].wait_recv()
    chalo[1][3].wait_recv()
    to_pair(1, 1, 1)
    to_own(1, 1)
    chalo[1][1].wait_recv()
    row_to_pair(1, 0)
    chalo[1][0].wait_recv()
    row_to_pair(1, 2)
    to_own(1, 0)
    to_own(1, 2)

    for i in range(CHAIN // 2):
        swap_copy(2 * i + core).wait_send()
        relay_copy(2 * i + core).wait_send()
    for j in range(CHAIN):

        @pl.when(dist < nz - 1)
        def _():
            ring_copy(j, False).wait_send()

    for r in range(3):
        give_tiles[0][r].wait_send()
        give_tiles[1][r].wait_send()
    for m in range(2):
        for copy in halo[m] + chalo[m]:
            copy.wait_send()
        for i in range(3):
            for copy in back[m][i]:
                copy.wait_send()
                copy.wait_recv()


def body(density, coupling, block_cols, block_count, energies):
    copies, halves, tile, _ = density.shape
    nr, slots, bs, _ = coupling.shape
    nk, nb = lax.axis_size("ket"), lax.axis_size("bra")
    total = block_cols.shape[0]
    any_space = pl.BlockSpec(memory_space=pl.ANY)
    vmem = pl.BlockSpec(memory_space=pltpu.VMEM)
    smem = pl.BlockSpec(memory_space=pltpu.SMEM)
    out = pl.pallas_call(
        functools.partial(kernel, nk, nb),
        out_shape=pltpu.VMEM((copies * halves, tile, tile), density.dtype),
        in_specs=[any_space, any_space, vmem, smem, smem],
        out_specs=vmem,
        scratch_shapes=[
            pltpu.VMEM((2, tile + 2 * bs, 2 * tile + 2 * bs), BF),
            pltpu.VMEM((2, tile + 2 * bs, 2 * tile + 2 * bs), BF),
            pltpu.VMEM((2, tile, tile), BF),
            pltpu.VMEM((nr, slots, bs, bs), BF),
            pltpu.VMEM((2 * nr, slots, bs, bs), BF),
            pltpu.VMEM((nr, bs, 3 * bs), BF),
            pltpu.VMEM((2 * nr, bs, 3 * bs), BF),
            pltpu.VMEM((nr, bs, 3 * bs), BF),
            pltpu.VMEM((2 * nr, bs, 3 * bs), BF),
            pltpu.VMEM((3 * nr, bs, 128), F32),
            pltpu.SemaphoreType.DMA((COPIES,)),
            pltpu.SemaphoreType.DMA((COPIES,)),
            pltpu.SemaphoreType.DMA((4,)),
        ],
        compiler_params=pltpu.CompilerParams(
            collective_id=0, has_side_effects=True, vmem_limit_bytes=52 << 20
        ),
        name="dissipator",
    )(density.reshape(copies * halves, tile, tile), coupling, energies.reshape(total, bs), block_cols, block_count)
    return out.reshape(density.shape)


def solution(mesh):
    return jax.shard_map(
        body,
        mesh=mesh,
        in_specs=(P(None, None, "ket", "bra"), P("bra", None, None, None), P(), P(), P()),
        out_specs=P(None, None, "ket", "bra"),
        check_vma=False,
    )
```

```python
import functools

import jax
import jax.numpy as jnp
from jax import lax
from jax.experimental import pallas as pl
from jax.experimental.pallas import tpu as pltpu
from jax.sharding import PartitionSpec as P

MESH = pl.DeviceIdType.MESH
BF = jnp.bfloat16
F32 = jnp.float32
CHAIN = 24
SWAP = 0
RELAY = SWAP + CHAIN
RING = RELAY + CHAIN
IN = RING + CHAIN
DHALO = IN + 6
CHALO = DHALO + 12
OUT = CHALO + 8
COPIES = OUT + 12
ORDER = (0, 2, 1)


def kernel(
    nk, nb, density, coupling, levels, block_cols, block_count, out,
    dext, cext, res, rraw, craw, orow, ocol, wrow, wcol, own_levels, ssem, rsem, lsem,
):
    nr, slots, bs, _ = coupling.shape
    tile = nr * bs
    total = block_cols.shape[1]
    k, b = lax.axis_index("ket"), lax.axis_index("bra")
    core, hi, lo, z, nz = k % 2, (k // 2) % 2, b % 2, b // 2, nb // 2
    flip = b + 1 - 2 * lo
    colour = (hi + lo) % 2
    keep, give = 2 * colour, 2 - 2 * colour
    pair = (k, flip)
    swap = (k + 2 - 4 * hi, flip)
    sibling = (k + 1 - 2 * core, b)
    up = ((k + nk - 1) % nk, core * b + (1 - core) * flip)
    down = ((k + 1) % nk, (1 - core) * b + core * flip)
    left, right = (k, (b + nb - 2) % nb), (k, (b + 2) % nb)
    after = (k, (b + 2 + core * (nb - 4)) % nb)
    away = (z + nz - (k // 2) % nz) % nz
    dist = (away + core * (2 * nz - 2 * away)) % nz
    source = dist == 0

    def cols(half):
        return pl.ds(pl.multiple_of(bs + half * tile, bs), tile)

    def rows(r):
        return pl.ds(r * bs, bs)

    mine, other = cols(lo), cols(1 - lo)
    first, last = pl.ds(bs, bs), pl.ds(nr * bs, bs)
    inner, across = pl.ds(bs, tile), pl.ds(bs, 2 * tile)
    above, below = pl.ds(0, bs), pl.ds((nr + 1) * bs, bs)
    lcol, rcol = pl.ds(bs, bs), pl.ds(2 * nr * bs, bs)
    lhalo, rhalo = pl.ds(0, bs), pl.ds((2 * nr + 1) * bs, bs)

    def remote(sends, receives, src, dst, device):
        return pltpu.make_async_remote_copy(
            src_ref=src, dst_ref=dst, send_sem=ssem.at[sends], recv_sem=rsem.at[receives],
            device_id=device, device_id_type=MESH,
        )

    own_tiles = [
        pltpu.make_async_copy(density.at[keep + m], dext.at[m, inner, mine], lsem.at[m]) for m in range(2)
    ]
    own_cols = pltpu.make_async_copy(coupling, craw.at[pl.ds(nr * lo, nr)], lsem.at[2])
    own_rows = pltpu.make_async_copy(craw.at[pl.ds(nr * core, nr)], rraw, lsem.at[3])
    own_cols.start()
    for copy in own_tiles:
        copy.start()

    barrier = pltpu.get_barrier_semaphore()
    for device in (pair, swap, up, down, left, right):
        pl.semaphore_signal(barrier, inc=1, device_id=device, device_id_type=MESH)

    def level_row(g):
        count = bs // 128
        return jnp.concatenate([levels[pl.ds(g * count + n, 1), :] for n in range(count)], axis=1)

    col_start = b // 2 * 2 * nr
    for p in range(3 * nr):
        g = k * nr + p if p < nr else col_start + p - nr
        own_levels[p] = jnp.transpose(jnp.broadcast_to(level_row(g), (128, bs)))
    pl.semaphore_wait(barrier, 6)

    parts = CHAIN // nr
    part = bs // parts

    def block_row(j):
        return j // parts * 2 % 3

    def chunk_rows(j):
        return pl.ds(pl.multiple_of(j % parts * part, part), part)

    def piece(ref, base, j):
        return ref.at[base + block_row(j), :, chunk_rows(j)]

    def swap_copy(j):
        return remote(SWAP + j, SWAP + j, piece(coupling, 0, j), piece(craw, nr * lo, j), swap)

    def relay_copy(j):
        got = piece(craw, nr * (1 - lo), j)
        return remote(RELAY + j, SWAP + j, got, got, sibling)

    def ring_copy(j, start):
        target = piece(rraw, 0, j)
        return remote(RING + j, RING + j, piece(craw, nr * core, j) if start else target, target, after)

    give_tiles = [
        [
            remote(IN + 3 * m + r, IN + 3 * m + r, density.at[give + m, rows(r)], dext.at[m, rows(r + 1), mine], pair)
            for r in range(3)
        ]
        for m in range(2)
    ]

    halo, chalo = [], []
    for m in range(2):
        moves = (
            (density.at[keep + m, rows(0)], dext.at[m, below, mine], up),
            (density.at[keep + m, rows(nr - 1)], dext.at[m, above, mine], down),
            (dext.at[m, first, other], dext.at[m, below, other], up),
            (dext.at[m, last, other], dext.at[m, above, other], down),
            (dext.at[m, inner, lcol], dext.at[m, inner, rhalo], left),
            (dext.at[m, inner, rcol], dext.at[m, inner, lhalo], right),
        )
        halo.append([remote(DHALO + 6 * m + n, DHALO + 6 * m + n, *move) for n, move in enumerate(moves)])
        moves = (
            (cext.at[m, first, across], cext.at[m, below, across], up),
            (cext.at[m, last, across], cext.at[m, above, across], down),
            (cext.at[m, inner, lcol], cext.at[m, inner, rhalo], left),
            (cext.at[m, inner, rcol], cext.at[m, inner, lhalo], right),
        )
        chalo.append([remote(CHALO + 4 * m + n, CHALO + 4 * m + n, *move) for n, move in enumerate(moves)])

    def order_chunk(raw, p, g, q, operator, weighted, at):
        held = [raw[p, s, at].astype(F32) for s in range(slots)]
        mine_levels = jnp.concatenate([own_levels[q, at]] * (bs // 128), axis=1)
        for n in range(3):
            there = level_row((g + total + n - 1) % total)
            x = mine_levels - there
            u = jnp.exp(jnp.abs(x) * -0.25)
            v = u * u
            v = v * v
            spectral = jnp.where(x >= 0, 1.0, v) / (1.0 + v) * u
            block = None
            for s in range(slots):
                used = (block_cols[s, g] == g + n - 1) & (s < block_count[g])
                term = held[s] * used.astype(jnp.int32).astype(F32)
                block = term if block is None else block + term
            operator[p, at, pl.ds(n * bs, bs)] = block.astype(BF)
            weighted[p, at, pl.ds(n * bs, bs)] = (block * spectral).astype(BF)

    def order_col(half, j):
        p = half * nr + block_row(j)
        order_chunk(craw, p, col_start + p, nr + p, ocol, wcol, chunk_rows(j))

    def order_row(j):
        p = block_row(j)
        order_chunk(rraw, p, k * nr + p, p, orow, wrow, chunk_rows(j))

    def taken(r, next_halo):
        give_tiles[0][r].wait_recv()
        for n in next_halo:
            halo[0][n].start()

    def due(j, at):
        return (j == at) | ((j == 0) & (at < 0)) | ((j == CHAIN) & (at > CHAIN))

    near = dist < nz // 2
    ready_source = source & (core == lo)

    def first_taken():
        halo[0][0].start()
        halo[0][1].start()
        taken(0, (2,))

    def relay_step(i, carry):
        @pl.when(i == CHAIN // 4)
        def _():
            first_taken()

        swap_copy(2 * i + core).wait_recv()
        relay_copy(2 * i + core).start()
        order_col(lo, 2 * i)
        order_col(lo, 2 * i + 1)
        return carry

    def step(j, carry):
        @pl.when(near & due(j, 12 - 5 * dist))
        def _():
            first_taken()

        @pl.when(due(j, 28 - 5 * dist))
        def _():
            taken(2, (3,))

        @pl.when(due(j, 44 - 5 * dist))
        def _():
            own_tiles[0].wait()
            taken(1, (4, 5))
            halo[1][0].start()
            halo[1][1].start()

        @pl.when(j < CHAIN)
        def _():
            @pl.when(ready_source)
            def _():
                ring_copy(j, True).start()

            @pl.when((near & (j % 2 == core)) | (jnp.logical_not(ready_source) & (j % 2 != core)))
            def _():
                swap_copy(j).wait_recv()

            @pl.when(near & (j % 2 == core))
            def _():
                relay_copy(j).start()

            @pl.when(source & (core != lo))
            def _():
                ring_copy(j, True).start()

            @pl.when(jnp.logical_not(ready_source))
            def _():
                order_col(1 - lo, j)

            @pl.when(dist != 0)
            def _():
                ring_copy(j, False).wait_recv()

            @pl.when((dist != 0) & (dist < nz - 1))
            def _():
                ring_copy(j, False).start()

            @pl.when(dist != 0)
            def _():
                order_row(j)

        return carry

    for i in range(CHAIN // 2):
        swap_copy(2 * i + core).start()
    for m in range(2):
        for r in ORDER:
            give_tiles[m][r].start()
    own_cols.wait()

    @pl.when(jnp.logical_not(near))
    def _():
        lax.fori_loop(0, CHAIN // 2, relay_step, 0)

    lax.fori_loop(0, CHAIN + 1, step, 0)

    @pl.when(near)
    def _():
        def own_col_step(j, carry):
            order_col(lo, j)
            return carry

        lax.fori_loop(0, CHAIN, own_col_step, 0)

    @pl.when(ready_source)
    def _():
        def other_col_step(j, carry):
            @pl.when(j % 2 != core)
            def _():
                swap_copy(j).wait_recv()

            order_col(1 - lo, j)
            return carry

        lax.fori_loop(0, CHAIN, other_col_step, 0)

    @pl.when(source)
    def _():
        own_rows.start()
        own_rows.wait()

        def own_step(j, carry):
            order_row(j)
            return carry

        lax.fori_loop(0, CHAIN, own_step, 0)

    def blocks(m, i, h, c, count, source_ref, row_op, col_op, store):
        base = pl.multiple_of((h * nr + c) * bs, bs)
        through_rows = jnp.dot(
            row_op[i], source_ref[m, pl.ds(i * bs, 3 * bs), pl.ds(pl.multiple_of(base + bs, bs), count * bs)],
            preferred_element_type=F32,
        )
        for j in range(count):
            through_cols = lax.dot_general(
                source_ref[m, rows(i + 1), pl.ds(pl.multiple_of(base + j * bs, bs), 3 * bs)], col_op[h * nr + c + j],
                (((1,), (1,)), ((), ())), preferred_element_type=F32,
            )
            store(j, through_rows[:, j * bs : (j + 1) * bs], through_cols)

    def commutand_row(m, i):
        def half(h, carry):
            def store(j, through_rows, through_cols):
                at = pl.multiple_of(h * tile + (j + 1) * bs, bs)
                cext[m, rows(i + 1), pl.ds(at, bs)] = (through_rows - through_cols).astype(BF)

            blocks(m, i, h, 0, nr, dext, wrow, wcol, store)
            return carry

        lax.fori_loop(0, 2, half, 0)

    inside, edge = pl.ds(pl.multiple_of(lo * bs, bs), 2 * bs), pl.ds(pl.multiple_of(2 * (1 - lo) * bs, bs), bs)
    back = [
        [
            [
                remote(OUT + n, OUT + n, res.at[m, rows(i), where], out.at[keep + m, rows(i), where], pair)
                for n, where in ((6 * m + 2 * i, inside), (6 * m + 2 * i + 1, edge))
            ]
            for i in range(3)
        ]
        for m in range(2)
    ]

    def to_pair(m, i, at_edge):
        start = 2 * (1 - lo) if at_edge else lo

        def store(j, through_rows, through_cols):
            at = pl.multiple_of((start + j) * bs, bs)
            res[m, rows(i), pl.ds(at, bs)] = (through_cols - through_rows).astype(BF)

        blocks(m, i, 1 - lo, start, 1 if at_edge else 2, cext, orow, ocol, store)
        back[m][i][at_edge].start()

    def to_own(m, i):
        def store(j, through_rows, through_cols):
            out[keep + m, rows(i), rows(j)] = (through_cols - through_rows).astype(BF)

        blocks(m, i, lo, 0, nr, cext, orow, ocol, store)

    def row_to_pair(m, i):
        to_pair(m, i, 0)
        to_pair(m, i, 1)

    def give_on(r, which):
        give_tiles[1][r].wait_recv()
        for n in which:
            halo[1][n].start()

    for copy in halo[0]:
        copy.wait_recv()
    commutand_row(0, 0)
    chalo[0][0].start()
    commutand_row(0, 2)
    chalo[0][1].start()
    commutand_row(0, 1)
    chalo[0][2].start()
    chalo[0][3].start()
    give_on(0, (2,))
    give_on(2, (3,))
    to_pair(0, 1, 0)
    own_tiles[1].wait()
    give_on(1, (4, 5))
    chalo[0][2].wait_recv()
    chalo[0][3].wait_recv()
    to_pair(0, 1, 1)
    to_own(0, 1)
    chalo[0][1].wait_recv()
    row_to_pair(0, 0)
    for copy in halo[1]:
        copy.wait_recv()
    commutand_row(1, 0)
    chalo[1][0].start()
    chalo[0][0].wait_recv()
    row_to_pair(0, 2)
    commutand_row(1, 2)
    chalo[1][1].start()
    commutand_row(1, 1)
    chalo[1][2].start()
    chalo[1][3].start()
    to_pair(1, 1, 0)
    to_own(0, 0)
    to_own(0, 2)
    chalo[1][2].wait_recv()
    chalo[1][3].wait_recv()
    to_pair(1, 1, 1)
    to_own(1, 1)
    chalo[1][1].wait_recv()
    row_to_pair(1, 0)
    chalo[1][0].wait_recv()
    row_to_pair(1, 2)
    to_own(1, 0)
    to_own(1, 2)

    for i in range(CHAIN // 2):
        swap_copy(2 * i + core).wait_send()
        relay_copy(2 * i + core).wait_send()
    for j in range(CHAIN):

        @pl.when(dist < nz - 1)
        def _():
            ring_copy(j, False).wait_send()

    for r in range(3):
        give_tiles[0][r].wait_send()
        give_tiles[1][r].wait_send()
    for m in range(2):
        for copy in halo[m] + chalo[m]:
            copy.wait_send()
        for i in range(3):
            for copy in back[m][i]:
                copy.wait_send()
                copy.wait_recv()


def body(density, coupling, block_cols, block_count, energies):
    copies, halves, tile, _ = density.shape
    nr, slots, bs, _ = coupling.shape
    nk, nb = lax.axis_size("ket"), lax.axis_size("bra")
    total = block_cols.shape[0]
    any_space = pl.BlockSpec(memory_space=pl.ANY)
    vmem = pl.BlockSpec(memory_space=pltpu.VMEM)
    smem = pl.BlockSpec(memory_space=pltpu.SMEM)
    out = pl.pallas_call(
        functools.partial(kernel, nk, nb),
        out_shape=pltpu.VMEM((copies * halves, tile, tile), density.dtype),
        in_specs=[any_space, any_space, vmem, smem, smem],
        out_specs=vmem,
        scratch_shapes=[
            pltpu.VMEM((2, tile + 2 * bs, 2 * tile + 2 * bs), BF),
            pltpu.VMEM((2, tile + 2 * bs, 2 * tile + 2 * bs), BF),
            pltpu.VMEM((2, tile, tile), BF),
            pltpu.VMEM((nr, slots, bs, bs), BF),
            pltpu.VMEM((2 * nr, slots, bs, bs), BF),
            pltpu.VMEM((nr, bs, 3 * bs), BF),
            pltpu.VMEM((2 * nr, bs, 3 * bs), BF),
            pltpu.VMEM((nr, bs, 3 * bs), BF),
            pltpu.VMEM((2 * nr, bs, 3 * bs), BF),
            pltpu.VMEM((3 * nr, bs, 128), F32),
            pltpu.SemaphoreType.DMA((COPIES,)),
            pltpu.SemaphoreType.DMA((COPIES,)),
            pltpu.SemaphoreType.DMA((4,)),
        ],
        compiler_params=pltpu.CompilerParams(
            collective_id=0, has_side_effects=True, vmem_limit_bytes=52 << 20
        ),
        name="dissipator",
    )(density.reshape(copies * halves, tile, tile), coupling, energies.reshape(total * bs // 128, 128), block_cols.T, block_count)
    return out.reshape(density.shape)


def solution(mesh):
    return jax.shard_map(
        body,
        mesh=mesh,
        in_specs=(P(None, None, "ket", "bra"), P("bra", None, None, None), P(), P(), P()),
        out_specs=P(None, None, "ket", "bra"),
        check_vma=False,
    )
```

```python
import functools

import jax
import jax.numpy as jnp
from jax import lax
from jax.experimental import pallas as pl
from jax.experimental.pallas import tpu as pltpu
from jax.sharding import PartitionSpec as P

MESH = pl.DeviceIdType.MESH
BF = jnp.bfloat16
F32 = jnp.float32
CHAIN = 24
SWAP = 0
RELAY = SWAP + CHAIN
RING = RELAY + CHAIN
IN = RING + CHAIN
DHALO = IN + 6
CHALO = DHALO + 12
OUT = CHALO + 8
COPIES = OUT + 12
ORDER = (0, 2, 1)


def kernel(
    nk, nb, density, coupling, levels, block_cols, block_count, out,
    dext, cext, res, rraw, craw, orow, ocol, wrow, wcol, own_levels, ssem, rsem, lsem,
):
    nr, slots, bs, _ = coupling.shape
    tile = nr * bs
    total = block_cols.shape[1]
    k, b = lax.axis_index("ket"), lax.axis_index("bra")
    core, hi, lo, z, nz = k % 2, (k // 2) % 2, b % 2, b // 2, nb // 2
    flip = b + 1 - 2 * lo
    colour = (hi + lo) % 2
    keep, give = 2 * colour, 2 - 2 * colour
    pair = (k, flip)
    swap = (k + 2 - 4 * hi, flip)
    sibling = (k + 1 - 2 * core, b)
    up = ((k + nk - 1) % nk, core * b + (1 - core) * flip)
    down = ((k + 1) % nk, (1 - core) * b + core * flip)
    left, right = (k, (b + nb - 2) % nb), (k, (b + 2) % nb)
    after = (k, (b + 2 + core * (nb - 4)) % nb)
    away = (z + nz - (k // 2) % nz) % nz
    dist = (away + core * (2 * nz - 2 * away)) % nz
    source = dist == 0

    def cols(half):
        return pl.ds(pl.multiple_of(bs + half * tile, bs), tile)

    def rows(r):
        return pl.ds(r * bs, bs)

    mine, other = cols(lo), cols(1 - lo)
    first, last = pl.ds(bs, bs), pl.ds(nr * bs, bs)
    inner, across = pl.ds(bs, tile), pl.ds(bs, 2 * tile)
    above, below = pl.ds(0, bs), pl.ds((nr + 1) * bs, bs)
    lcol, rcol = pl.ds(bs, bs), pl.ds(2 * nr * bs, bs)
    lhalo, rhalo = pl.ds(0, bs), pl.ds((2 * nr + 1) * bs, bs)

    def remote(sends, receives, src, dst, device):
        return pltpu.make_async_remote_copy(
            src_ref=src, dst_ref=dst, send_sem=ssem.at[sends], recv_sem=rsem.at[receives],
            device_id=device, device_id_type=MESH,
        )

    own_tiles = [
        pltpu.make_async_copy(density.at[keep + m], dext.at[m, inner, mine], lsem.at[m]) for m in range(2)
    ]
    own_cols = pltpu.make_async_copy(coupling, craw.at[pl.ds(nr * lo, nr)], lsem.at[2])
    own_rows = pltpu.make_async_copy(craw.at[pl.ds(nr * core, nr)], rraw, lsem.at[3])
    own_cols.start()
    for copy in own_tiles:
        copy.start()

    barrier = pltpu.get_barrier_semaphore()
    for device in (pair, swap, up, down, left, right):
        pl.semaphore_signal(barrier, inc=1, device_id=device, device_id_type=MESH)

    def level_row(g):
        count = bs // 128
        return jnp.concatenate([levels[pl.ds(g * count + n, 1), :] for n in range(count)], axis=1)

    col_start = b // 2 * 2 * nr
    for p in range(3 * nr):
        g = k * nr + p if p < nr else col_start + p - nr
        own_levels[p] = jnp.transpose(jnp.broadcast_to(level_row(g), (128, bs)))
    pl.semaphore_wait(barrier, 6)

    parts = CHAIN // nr
    part = bs // parts

    def block_row(j):
        return j // parts * 2 % 3

    def chunk_rows(j):
        return pl.ds(pl.multiple_of(j % parts * part, part), part)

    def piece(ref, base, j):
        return ref.at[base + block_row(j), :, chunk_rows(j)]

    def swap_copy(j):
        return remote(SWAP + j, SWAP + j, piece(coupling, 0, j), piece(craw, nr * lo, j), swap)

    def relay_copy(j):
        got = piece(craw, nr * (1 - lo), j)
        return remote(RELAY + j, SWAP + j, got, got, sibling)

    def ring_copy(j, start):
        target = piece(rraw, 0, j)
        return remote(RING + j, RING + j, piece(craw, nr * core, j) if start else target, target, after)

    give_tiles = [
        [
            remote(IN + 3 * m + r, IN + 3 * m + r, density.at[give + m, rows(r)], dext.at[m, rows(r + 1), mine], pair)
            for r in range(3)
        ]
        for m in range(2)
    ]

    halo, chalo = [], []
    for m in range(2):
        moves = (
            (density.at[keep + m, rows(0)], dext.at[m, below, mine], up),
            (density.at[keep + m, rows(nr - 1)], dext.at[m, above, mine], down),
            (dext.at[m, first, other], dext.at[m, below, other], up),
            (dext.at[m, last, other], dext.at[m, above, other], down),
            (dext.at[m, inner, lcol], dext.at[m, inner, rhalo], left),
            (dext.at[m, inner, rcol], dext.at[m, inner, lhalo], right),
        )
        halo.append([remote(DHALO + 6 * m + n, DHALO + 6 * m + n, *move) for n, move in enumerate(moves)])
        moves = (
            (cext.at[m, first, across], cext.at[m, below, across], up),
            (cext.at[m, last, across], cext.at[m, above, across], down),
            (cext.at[m, inner, lcol], cext.at[m, inner, rhalo], left),
            (cext.at[m, inner, rcol], cext.at[m, inner, lhalo], right),
        )
        chalo.append([remote(CHALO + 4 * m + n, CHALO + 4 * m + n, *move) for n, move in enumerate(moves)])

    def order_chunk(raw, p, g, q, operator, weighted, at):
        held = [raw[p, s, at].astype(F32) for s in range(slots)]
        mine_levels = jnp.concatenate([own_levels[q, at]] * (bs // 128), axis=1)
        for n in range(3):
            there = level_row((g + total + n - 1) % total)
            x = mine_levels - there
            u = jnp.exp(jnp.abs(x) * -0.25)
            v = u * u
            v = v * v
            spectral = jnp.where(x >= 0, 1.0, v) / (1.0 + v) * u
            block = None
            for s in range(slots):
                used = (block_cols[s, g] == g + n - 1) & (s < block_count[g])
                term = held[s] * used.astype(jnp.int32).astype(F32)
                block = term if block is None else block + term
            operator[p, at, pl.ds(n * bs, bs)] = block.astype(BF)
            weighted[p, at, pl.ds(n * bs, bs)] = (block * spectral).astype(BF)

    def order_col(half, j):
        p = half * nr + block_row(j)
        order_chunk(craw, p, col_start + p, nr + p, ocol, wcol, chunk_rows(j))

    def order_row(j):
        p = block_row(j)
        order_chunk(rraw, p, k * nr + p, p, orow, wrow, chunk_rows(j))

    def taken(r, next_halo):
        give_tiles[0][r].wait_recv()
        for n in next_halo:
            halo[0][n].start()

    def due(j, at):
        return (j == at) | ((j == 0) & (at < 0)) | ((j == CHAIN) & (at > CHAIN))

    near = dist < nz // 2
    ready_source = source & (core == lo)

    def first_taken():
        halo[0][0].start()
        halo[0][1].start()
        taken(0, (2,))

    def relay_step(i, carry):
        @pl.when(i == CHAIN // 4)
        def _():
            first_taken()

        swap_copy(2 * i + core).wait_recv()
        relay_copy(2 * i + core).start()
        order_col(lo, 2 * i)
        order_col(lo, 2 * i + 1)
        return carry

    def step(j, carry):
        @pl.when(near & due(j, 12 - 5 * dist))
        def _():
            first_taken()

        @pl.when(due(j, 28 - 5 * dist))
        def _():
            taken(2, (3,))

        @pl.when(due(j, 44 - 5 * dist))
        def _():
            own_tiles[0].wait()
            taken(1, (4, 5))
            halo[1][0].start()
            halo[1][1].start()

        @pl.when(j < CHAIN)
        def _():
            @pl.when(ready_source)
            def _():
                ring_copy(j, True).start()

            @pl.when((near & (j % 2 == core)) | (jnp.logical_not(ready_source) & (j % 2 != core)))
            def _():
                swap_copy(j).wait_recv()

            @pl.when(near & (j % 2 == core))
            def _():
                relay_copy(j).start()

            @pl.when(source & (core != lo))
            def _():
                ring_copy(j, True).start()

            @pl.when(jnp.logical_not(ready_source))
            def _():
                order_col(1 - lo, j)

            @pl.when(dist != 0)
            def _():
                ring_copy(j, False).wait_recv()

            @pl.when((dist != 0) & (dist < nz - 1))
            def _():
                ring_copy(j, False).start()

            @pl.when(dist != 0)
            def _():
                order_row(j)

        return carry

    for i in range(CHAIN // 2):
        swap_copy(2 * i + core).start()
    for m in range(2):
        for r in ORDER:
            give_tiles[m][r].start()
    own_cols.wait()

    @pl.when(jnp.logical_not(near))
    def _():
        lax.fori_loop(0, CHAIN // 2, relay_step, 0)

    lax.fori_loop(0, CHAIN + 1, step, 0)

    @pl.when(near)
    def _():
        def own_col_step(j, carry):
            order_col(lo, j)
            return carry

        lax.fori_loop(0, CHAIN, own_col_step, 0)

    @pl.when(ready_source)
    def _():
        def other_col_step(j, carry):
            @pl.when(j % 2 != core)
            def _():
                swap_copy(j).wait_recv()

            order_col(1 - lo, j)
            return carry

        lax.fori_loop(0, CHAIN, other_col_step, 0)

    @pl.when(source)
    def _():
        own_rows.start()
        own_rows.wait()

        def own_step(j, carry):
            order_row(j)
            return carry

        lax.fori_loop(0, CHAIN, own_step, 0)

    def blocks(m, i, h, c, count, source_ref, row_op, col_op, store):
        base = pl.multiple_of((h * nr + c) * bs, bs)
        through_rows = jnp.dot(
            row_op[i], source_ref[m, pl.ds(i * bs, 3 * bs), pl.ds(pl.multiple_of(base + bs, bs), count * bs)],
            preferred_element_type=F32,
        )
        for j in range(count):
            through_cols = lax.dot_general(
                source_ref[m, rows(i + 1), pl.ds(pl.multiple_of(base + j * bs, bs), 3 * bs)], col_op[h * nr + c + j],
                (((1,), (1,)), ((), ())), preferred_element_type=F32,
            )
            store(j, through_rows[:, j * bs : (j + 1) * bs], through_cols)

    def commutand_row(m, i):
        def half(h, carry):
            def store(j, through_rows, through_cols):
                at = pl.multiple_of(h * tile + (j + 1) * bs, bs)
                cext[m, rows(i + 1), pl.ds(at, bs)] = (through_rows - through_cols).astype(BF)

            blocks(m, i, h, 0, nr, dext, wrow, wcol, store)
            return carry

        lax.fori_loop(0, 2, half, 0)

    inside, edge = pl.ds(pl.multiple_of(lo * bs, bs), 2 * bs), pl.ds(pl.multiple_of(2 * (1 - lo) * bs, bs), bs)
    back = [
        [
            [
                remote(OUT + n, OUT + n, res.at[m, rows(i), where], out.at[keep + m, rows(i), where], pair)
                for n, where in ((6 * m + 2 * i, inside), (6 * m + 2 * i + 1, edge))
            ]
            for i in range(3)
        ]
        for m in range(2)
    ]

    def to_pair(m, i, at_edge):
        start = 2 * (1 - lo) if at_edge else lo

        def store(j, through_rows, through_cols):
            at = pl.multiple_of((start + j) * bs, bs)
            res[m, rows(i), pl.ds(at, bs)] = (through_cols - through_rows).astype(BF)

        blocks(m, i, 1 - lo, start, 1 if at_edge else 2, cext, orow, ocol, store)
        back[m][i][at_edge].start()

    def to_own(m, i):
        def store(j, through_rows, through_cols):
            out[keep + m, rows(i), rows(j)] = (through_cols - through_rows).astype(BF)

        blocks(m, i, lo, 0, nr, cext, orow, ocol, store)

    def row_to_pair(m, i):
        to_pair(m, i, 0)
        to_pair(m, i, 1)

    def give_on(r, which):
        give_tiles[1][r].wait_recv()
        for n in which:
            halo[1][n].start()

    give_on(0, (2,))
    give_on(2, (3,))
    for copy in halo[0]:
        copy.wait_recv()
    commutand_row(0, 0)
    chalo[0][0].start()
    commutand_row(0, 2)
    chalo[0][1].start()
    own_tiles[1].wait()
    give_on(1, (4, 5))
    commutand_row(0, 1)
    chalo[0][2].start()
    chalo[0][3].start()
    to_pair(0, 1, 0)
    chalo[0][2].wait_recv()
    chalo[0][3].wait_recv()
    to_pair(0, 1, 1)
    to_own(0, 1)
    chalo[0][1].wait_recv()
    row_to_pair(0, 0)
    for copy in halo[1]:
        copy.wait_recv()
    commutand_row(1, 0)
    chalo[1][0].start()
    chalo[0][0].wait_recv()
    row_to_pair(0, 2)
    commutand_row(1, 2)
    chalo[1][1].start()
    commutand_row(1, 1)
    chalo[1][2].start()
    chalo[1][3].start()
    to_pair(1, 1, 0)
    to_own(0, 0)
    to_own(0, 2)
    chalo[1][2].wait_recv()
    chalo[1][3].wait_recv()
    to_pair(1, 1, 1)
    to_own(1, 1)
    chalo[1][1].wait_recv()
    row_to_pair(1, 0)
    chalo[1][0].wait_recv()
    row_to_pair(1, 2)
    to_own(1, 0)
    to_own(1, 2)

    for i in range(CHAIN // 2):
        swap_copy(2 * i + core).wait_send()
        relay_copy(2 * i + core).wait_send()
    for j in range(CHAIN):

        @pl.when(dist < nz - 1)
        def _():
            ring_copy(j, False).wait_send()

    for r in range(3):
        give_tiles[0][r].wait_send()
        give_tiles[1][r].wait_send()
    for m in range(2):
        for copy in halo[m] + chalo[m]:
            copy.wait_send()
        for i in range(3):
            for copy in back[m][i]:
                copy.wait_send()
                copy.wait_recv()


def body(density, coupling, block_cols, block_count, energies):
    copies, halves, tile, _ = density.shape
    nr, slots, bs, _ = coupling.shape
    nk, nb = lax.axis_size("ket"), lax.axis_size("bra")
    total = block_cols.shape[0]
    any_space = pl.BlockSpec(memory_space=pl.ANY)
    vmem = pl.BlockSpec(memory_space=pltpu.VMEM)
    smem = pl.BlockSpec(memory_space=pltpu.SMEM)
    out = pl.pallas_call(
        functools.partial(kernel, nk, nb),
        out_shape=pltpu.VMEM((copies * halves, tile, tile), density.dtype),
        in_specs=[any_space, any_space, vmem, smem, smem],
        out_specs=vmem,
        scratch_shapes=[
            pltpu.VMEM((2, tile + 2 * bs, 2 * tile + 2 * bs), BF),
            pltpu.VMEM((2, tile + 2 * bs, 2 * tile + 2 * bs), BF),
            pltpu.VMEM((2, tile, tile), BF),
            pltpu.VMEM((nr, slots, bs, bs), BF),
            pltpu.VMEM((2 * nr, slots, bs, bs), BF),
            pltpu.VMEM((nr, bs, 3 * bs), BF),
            pltpu.VMEM((2 * nr, bs, 3 * bs), BF),
            pltpu.VMEM((nr, bs, 3 * bs), BF),
            pltpu.VMEM((2 * nr, bs, 3 * bs), BF),
            pltpu.VMEM((3 * nr, bs, 128), F32),
            pltpu.SemaphoreType.DMA((COPIES,)),
            pltpu.SemaphoreType.DMA((COPIES,)),
            pltpu.SemaphoreType.DMA((4,)),
        ],
        compiler_params=pltpu.CompilerParams(
            collective_id=0, has_side_effects=True, vmem_limit_bytes=52 << 20
        ),
        name="dissipator",
    )(density.reshape(copies * halves, tile, tile), coupling, energies.reshape(total * bs // 128, 128), block_cols.T, block_count)
    return out.reshape(density.shape)


def solution(mesh):
    return jax.shard_map(
        body,
        mesh=mesh,
        in_specs=(P(None, None, "ket", "bra"), P("bra", None, None, None), P(), P(), P()),
        out_specs=P(None, None, "ket", "bra"),
        check_vma=False,
    )
```
